32 devices in a mesh: seq: 8 (over z, y), batch: 4 (over x, core).
Axes of the slice: x: 2, y: 2, z: 4, core: 2. Of those that a mesh axis runs over, the one named last changes fastest.
Arguments:
- tokens: bfloat16 [16, 1024, 896], P('batch', 'seq'), may hold values from -6 to 6
- doc_start: int32 [16, 1024], P('batch', 'seq'), may hold values from 0 to 1023, as said below
- neighbours: bfloat16 [16, 16, 256, 896], P('batch', 'seq'), may hold values from -6 to 6
- qkv_weight: bfloat16 [896, 6144], P(None, ('seq', 'batch')), may hold values from -0.25 to 0.25
- out_weight: bfloat16 [1024, 1792], P(None, ('seq', 'batch')), may hold values from -0.5 to 0.5
- ff_in: bfloat16 [896, 3584], P(None, ('seq', 'batch')), may hold values from -0.1875 to 0.1875
- ff_out: bfloat16 [3584, 896], P(('seq', 'batch')), may hold values from -0.09375 to 0.09375
- gains: float32 [3, 896], replicated, may hold values from 0.25 to 1.75
- cotangent: bfloat16 [16, 1024, 896], P('batch', 'seq'), may hold values from -6 to 6
Outputs:
- output: bfloat16 [16, 1024, 896], P('batch', 'seq')
- grad_tokens: float32 [16, 1024, 896], P('batch', 'seq')
- grad_neighbours: float32 [16, 16, 256, 896], P('batch', 'seq')
- grad_qkv_weight: float32 [896, 6144], P(None, ('seq', 'batch'))
- grad_out_weight: float32 [1024, 1792], P(None, ('seq', 'batch'))
- grad_ff_in: float32 [896, 3584], P(None, ('seq', 'batch'))
- grad_ff_out: float32 [3584, 896], P(('seq', 'batch'))
- grad_gains: float32 [3, 896], replicated
The draws below stay inside these ranges and needn't reach their ends.
Inputs may be any that keep to these rules, and one draw needn't show every extreme that they name: doc_start[b, p] is where the document holding token p of sequence b begins: doc_start[b, 0] = 0, and doc_start[b, p] is p or doc_start[b, p - 1]. The last position of every sequence begins a document of one token.
All inputs are finite; a program needn't handle non-finite values.
Results may differ from the reference program's by a relative error of at most 0.025.
The reference program's roundings to bfloat16 on the way count: a program that leaves them out, or rounds other values in their place, can miss the bound.
Values may be sent and summed in bfloat16 or wider, within the bound.
No kernel may reach another device: no remote copies, remote signals or barrier semaphores. Data moves between devices by JAX's collectives and lax.ppermute only.
A program may use at most 384 MiB of HBM per device.

```python
import math
import jax
import jax.numpy as jnp
from jax import lax

D = 896
HEADS = 16
HEAD = 64
FF = 3584
SPAN = 64
ATT = 1024
LEN = 1024
SEQS = 16
SPANS = 16
RETRIEVED = 256


def draw_doc_start(key, part):
    level_key, mark_key = jax.random.split(jax.random.fold_in(key, 11))
    level = jax.random.randint(level_key, (SEQS, 1), 0, 4)
    spacing = jnp.maximum(LEN // 2 >> 2 * level, 2)
    marks = jax.random.randint(mark_key, (SEQS, LEN), 0, 1 << 30)
    place = jnp.arange(LEN, dtype=jnp.int32)[None, :]
    begins = (marks % spacing == 0) | (place == 0) | (place == LEN - 1)
    marked = jnp.where(begins, place, 0)
    return lax.cummax(marked, axis=1).astype(jnp.int32)


def levels(key, shape, cuts, low, top_value):
    def one(dim, parts):
        heights = jax.random.uniform(jax.random.fold_in(jax.random.fold_in(key, 6), dim), (parts,), jnp.float32, low / len(cuts), top_value / len(cuts))
        return jnp.repeat(jnp.exp(heights), shape[dim] // parts).reshape((-1,) + (1,) * (len(shape) - dim - 1))

    level = one(*cuts[0])
    for cut in cuts[1:]:
        level = level * one(*cut)
    return level


def bell_draw(own_key, dims, width, limit, shards=(), kind=jnp.bfloat16):
    drawn = jax.random.normal(own_key, dims, jnp.float32) * width
    if len(shards) > 0:
        drawn = levels(own_key, dims, shards, -0.22, 0.18) * drawn
    return jnp.clip(drawn, min=-limit, max=limit).astype(kind)


def setup_inputs(seed: int = 0) -> dict:
    splits = jax.random.split(jax.random.key(seed), 10)
    tokens = bell_draw(splits[0], (SEQS, LEN, D), 1.0, 6.0, ((0, 4), (1, 8)))
    doc_start = draw_doc_start(jax.random.fold_in(splits[9], 71), 0)
    neighbours = bell_draw(splits[2], (SEQS, SPANS, RETRIEVED, D), 1.0, 6.0, ((0, 4), (1, 8)))
    qkv_weight = bell_draw(splits[3], (D, 6 * ATT), (D // 2) ** -0.5, 0.25, ((1, 32),))
    out_weight = bell_draw(splits[4], (ATT, 2 * D), (ATT // 8) ** -0.5, 0.5, ((1, 32),))
    ff_in = bell_draw(splits[5], (D, FF), D ** -0.5, 0.1875, ((1, 32),))
    ff_out = bell_draw(splits[6], (FF, D), FF ** -0.5, 0.09375, ((0, 32),))
    gains = jnp.clip(1.0 + 0.15 * jax.random.normal(splits[7], (3, D), jnp.float32), 0.25, 1.75)
    cotangent = bell_draw(splits[8], (SEQS, LEN, D), 1.0, 6.0, ((0, 4), (1, 8)))
    return dict(tokens=tokens, doc_start=doc_start, neighbours=neighbours, qkv_weight=qkv_weight, out_weight=out_weight, ff_in=ff_in, ff_out=ff_out, gains=gains, cotangent=cotangent)


highest = lax.Precision.HIGHEST
score_scale = 0.125
gelu_coef = math.sqrt(2.0 / math.pi)
norm_eps = 1e-05

@jax.custom_vjp
def low(v):
    return lax.optimization_barrier(v.astype(jnp.bfloat16)).astype(jnp.float32)

@jax.custom_vjp
def low_back(v):
    return v

def low_keep(v):
    return (low(v), None)

def low_pass(kept, grad):
    return (grad,)

def back_keep(v):
    return (v, None)

def back_low(kept, grad):
    return (low(grad),)
low.defvjp(low_keep, low_pass)
low_back.defvjp(back_keep, back_low)

def matmul(left, right):
    return jnp.dot(left, right, precision=highest)

def rms_norm(values, gain):
    return values * lax.rsqrt(lax.optimization_barrier(jnp.mean(values * values, axis=-1, keepdims=True)) + norm_eps) * gain

def heads_of(values):
    return values.reshape(values.shape[:-1] + (HEADS, HEAD))

def rope_tables(relative):
    half_size = HEAD // 2
    frequency = jnp.exp(jnp.arange(half_size, dtype=jnp.float32) * (-math.log(10000.0) / half_size))
    angles = relative[..., None] * frequency
    return (jnp.cos(angles), jnp.sin(angles))

def rotate(values, cosine_table, sine_table, turn_sign):
    full_shape = values.shape
    split_heads = heads_of(values)
    half_size = HEAD // 2
    first_half = split_heads[..., :half_size]
    second_half = split_heads[..., half_size:]
    cosines = cosine_table[..., None, :]
    sines_now = sine_table[..., None, :] * turn_sign
    turned = jnp.concatenate([first_half * cosines - second_half * sines_now, first_half * sines_now + second_half * cosines], axis=-1)
    return turned.reshape(full_shape)

def gelu_tanh(values):
    return 0.5 * values * (1.0 + jnp.tanh(gelu_coef * (values + 0.044715 * values * values * values)))

def layer_forward(resid_in, neighbour_rows, qkv_w, out_w, w_in, w_out, gain_rows, start_rows):
    seq_len, model_width = resid_in.shape
    att_width = HEADS * HEAD
    position = jnp.arange(seq_len, dtype=jnp.int32)
    cosine_table, sine_table = rope_tables((position - start_rows).astype(jnp.float32))
    input_one = low(rms_norm(resid_in, gain_rows[0]))
    proj_self = matmul(input_one, qkv_w[:, :3 * att_width])
    query_rot = low(rotate(low_back(proj_self[:, :att_width]), cosine_table, sine_table, 1.0))
    key_rot = low(rotate(low_back(proj_self[:, att_width:2 * att_width]), cosine_table, sine_table, 1.0))
    value_self = low(low_back(proj_self[:, 2 * att_width:]))
    key_heads = heads_of(key_rot)
    value_heads = heads_of(value_self)

    def self_block(block_inputs):
        query_block, start_block, place_block = block_inputs
        scores = low_back(jnp.einsum('qhd,khd->hqk', heads_of(query_block), key_heads, precision=highest) * score_scale)
        allowed = (position[None, :] >= start_block[:, None]) & (position[None, :] <= place_block[:, None])
        scores = jnp.where(allowed[None], scores, -1e+30)
        attn_probs = jax.nn.softmax(scores, axis=-1)
        mixed_rows = jnp.einsum('hqk,khd->qhd', low(attn_probs), value_heads, precision=highest)
        return mixed_rows.reshape(query_block.shape)
    attn_block = min(512, seq_len)
    block_count = seq_len // attn_block
    blocks = lax.map(jax.checkpoint(self_block), (query_rot.reshape(block_count, attn_block, att_width), start_rows.reshape(block_count, attn_block), position.reshape(block_count, attn_block)))
    attn_self = low(low_back(blocks.reshape(seq_len, att_width)))
    resid_mid = resid_in + low_back(matmul(attn_self, out_w[:, :model_width]))
    input_two = low(rms_norm(resid_mid, gain_rows[1]))
    query_cross = low(low_back(matmul(input_two, qkv_w[:, 3 * att_width:4 * att_width])))
    span_count = neighbour_rows.shape[0]
    retrieved = neighbour_rows.shape[1]
    proj_cross = matmul(neighbour_rows.reshape(span_count * retrieved, model_width), qkv_w[:, 4 * att_width:]).reshape(span_count, retrieved, 2 * att_width)
    key_cross = low(low_back(proj_cross[..., :att_width]))
    value_cross = low(low_back(proj_cross[..., att_width:]))
    empty_group = jnp.zeros((1, retrieved, att_width), jnp.float32)
    ext_keys = heads_of(jnp.concatenate([empty_group, key_cross], axis=0))
    ext_values = heads_of(jnp.concatenate([empty_group, value_cross], axis=0))
    pad_front = jnp.zeros((1, att_width), jnp.float32)
    pad_back = jnp.zeros((SPAN - 1, att_width), jnp.float32)
    query_groups = heads_of(jnp.concatenate([pad_front, query_cross, pad_back], axis=0).reshape(span_count + 1, SPAN, att_width))
    scores_cross = low_back(jnp.einsum('gqhd,grhd->ghqr', query_groups, ext_keys, precision=highest) * score_scale)
    probs_cross = jax.nn.softmax(scores_cross, axis=-1)
    mixed_cross = jnp.einsum('ghqr,grhd->gqhd', low(probs_cross), ext_values, precision=highest)
    mixed_cross = mixed_cross.reshape((span_count + 1) * SPAN, att_width)[1:seq_len + 1]
    span_of = (position + 1) // SPAN - 1
    valid_rows = ((span_of >= 0) & (start_rows <= span_of * SPAN + SPAN - 1)).astype(jnp.float32)
    attn_cross = low(low_back(mixed_cross * valid_rows[:, None]))
    resid_late = resid_mid + low_back(matmul(attn_cross, out_w[:, model_width:]))
    input_three = low(rms_norm(resid_late, gain_rows[2]))
    pre_act = low_back(matmul(input_three, w_in))
    activated = low(gelu_tanh(pre_act))
    return resid_late + low_back(matmul(activated, w_out))

def reference(tokens, doc_start, neighbours, qkv_weight, out_weight, ff_in, ff_out, gains, cotangent):
    matrices = (qkv_weight.astype(jnp.float32), out_weight.astype(jnp.float32), ff_in.astype(jnp.float32), ff_out.astype(jnp.float32))
    gain_rows = gains.astype(jnp.float32)

    def seq_step(totals, step_inputs):
        token_rows, start_rows, neighbour_rows, cotangent_rows = step_inputs

        def apply_layer(resid_in, nb_rows, qkv_w, out_w, w_in, w_out, gain_now):
            return layer_forward(resid_in, nb_rows, qkv_w, out_w, w_in, w_out, gain_now, start_rows)
        result, pullback = jax.vjp(apply_layer, token_rows.astype(jnp.float32), neighbour_rows.astype(jnp.float32), matrices[0], matrices[1], matrices[2], matrices[3], gain_rows)
        grads = pullback(cotangent_rows.astype(jnp.float32))
        totals = tuple((total + grad_part for total, grad_part in zip(totals, grads[2:])))
        return (totals, (result.astype(jnp.bfloat16), grads[0], grads[1]))
    initial = tuple((jnp.zeros(matrix.shape, jnp.float32) for matrix in matrices + (gain_rows,)))
    totals, (output, grad_tokens, grad_neighbours) = lax.scan(seq_step, initial, (tokens, doc_start, neighbours, cotangent))
    return (output, grad_tokens, grad_neighbours, totals[0], totals[1], totals[2], totals[3], totals[4])
```

```python
import functools
import math

import jax
import jax.numpy as jnp
from jax import lax
from jax.experimental import pallas as pl
from jax.experimental.pallas import tpu as pltpu
from jax.sharding import PartitionSpec as P

HEADS = 16
HEAD = 64
SPAN = 64
ATT = HEADS * HEAD
SHIFT = SPAN - 1
BOTH = ("seq", "batch")

score_scale = 0.125
gelu_coef = math.sqrt(2.0 / math.pi)
norm_eps = 1e-05
BF = jnp.bfloat16
F32 = jnp.float32

NT = (((1,), (1,)), ((), ()))
NN = (((1,), (0,)), ((), ()))
TN = (((0,), (0,)), ((), ()))


def mm(left, right, dims):
    return lax.dot_general(left, right, dims, preferred_element_type=F32)


def params(**kw):
    return pltpu.CompilerParams(vmem_limit_bytes=60 * 1024 * 1024, **kw)


def cost(flops, size, exps=0):
    return pl.CostEstimate(flops=int(flops), bytes_accessed=int(size), transcendentals=int(exps))


def half_swap(values):
    width = values.shape[-1]
    half = HEAD // 2
    lane = lax.broadcasted_iota(jnp.int32, values.shape, 1)
    if width % 128 == 0:
        ahead = pltpu.roll(values, width - half, 1)
        behind = pltpu.roll(values, half, 1)
    else:
        ahead = jnp.concatenate([values[:, half:], values[:, :half]], axis=1)
        behind = jnp.concatenate([values[:, -half:], values[:, :-half]], axis=1)
    return jnp.where(lane % HEAD < half, ahead, behind)


def proj_kernel(x_ref, wq_ref, wk_ref, wv_ref, cos_ref, sin_ref, out_ref):
    groups, _, width3 = out_ref.shape
    width = width3 // 3
    x = x_ref[...]
    for part, w_ref in enumerate((wq_ref, wk_ref, wv_ref)):
        acc = mm(x, w_ref[...], NT)
        for g in range(groups):
            piece = acc[:, g * width : (g + 1) * width]
            if part < 2:
                piece = piece * cos_ref[...] + half_swap(piece) * sin_ref[...]
            out_ref[g, :, part * width : (part + 1) * width] = piece.astype(BF)


def project_self(x, qkv_t, cos_rows, sin_rows, parts):
    rows, model = x.shape
    width = ATT // parts
    groups = 2 if width % 128 == 0 else 1
    steps = parts // groups
    wide = groups * width
    full = lambda i: (0, 0)
    return pl.pallas_call(
        proj_kernel,
        grid=(steps,),
        in_specs=[
            pl.BlockSpec((rows, model), full),
            pl.BlockSpec((wide, model), lambda i: (i, 0)),
            pl.BlockSpec((wide, model), lambda i: (steps + i, 0)),
            pl.BlockSpec((wide, model), lambda i: (2 * steps + i, 0)),
            pl.BlockSpec((rows, width), full),
            pl.BlockSpec((rows, width), full),
        ],
        out_specs=pl.BlockSpec((groups, rows, 3 * width), lambda i: (i, 0, 0)),
        out_shape=jax.ShapeDtypeStruct((parts, rows, 3 * width), BF),
        compiler_params=params(),
        cost_estimate=cost(2 * rows * model * 3 * ATT, 2 * (3 * ATT * model + rows * 4 * ATT)),
        name="proj_self",
    )(x, qkv_t, qkv_t, qkv_t, cos_rows, sin_rows)


def head_mask(shape, head):
    lane = lax.broadcasted_iota(jnp.int32, shape, 1)
    return lane // HEAD == head


def key_segments(block, block_rows, length, tail):
    stop = (block + 1) * block_rows
    if stop + tail > length:
        return [(0, length)]
    return [(0, stop), (length - tail, length)]


def segment_allowed(segment, q_pos, q_doc, length):
    start, stop = segment
    index = lax.broadcasted_iota(jnp.int32, (1, stop - start), 1) + start
    k_pos = jnp.where(index + SHIFT >= length, index + SHIFT - length, index + SHIFT)
    return (k_pos >= q_doc) & (k_pos <= q_pos)


def query_place(block, block_rows, length):
    index = lax.broadcasted_iota(jnp.int32, (block_rows, 1), 0) + block * block_rows
    return jnp.where(index + SHIFT >= length, index + SHIFT - length, index + SHIFT)


def masked_scores(q_h, k, segs, allowed):
    return [
        jnp.where(ok, mm(q_h, k[a:b], NT), -1e30) for (a, b), ok in zip(segs, allowed)
    ]


def soft(scores):
    top = functools.reduce(jnp.maximum, [jnp.max(s, axis=1, keepdims=True) for s in scores])
    weights = [jnp.exp(s - top) for s in scores]
    total = sum(jnp.sum(e, axis=1, keepdims=True) for e in weights)
    return weights, 1.0 / total


def attn_fwd_kernel(qkv_ref, doc_ref, out_ref, *, block_rows, tail):
    parts, _, tok, width3 = qkv_ref.shape
    width = width3 // 3
    length = parts * tok
    heads = width // HEAD
    per = block_rows // tok
    k = qkv_ref[:, 0, :, width : 2 * width].reshape(length, width)
    v = qkv_ref[:, 0, :, 2 * width :].reshape(length, width)
    for block in range(length // block_rows):
        rows = slice(block * per, (block + 1) * per)
        q = qkv_ref[rows, 0, :, :width].reshape(block_rows, width) * BF(score_scale)
        q_doc = doc_ref[0, block * block_rows : (block + 1) * block_rows, :]
        q_pos = query_place(block, block_rows, length)
        segs = key_segments(block, block_rows, length, tail)
        allowed = [segment_allowed(s, q_pos, q_doc, length) for s in segs]
        mixed = None
        for head in range(heads):
            q_h = jnp.where(head_mask(q.shape, head), q, BF(0)) if heads > 1 else q
            weights, inv = soft(masked_scores(q_h, k, segs, allowed))
            piece = sum(mm(e.astype(BF), v[a:b], NN) for e, (a, b) in zip(weights, segs)) * inv
            mixed = piece if mixed is None else jnp.where(
                head_mask(piece.shape, head), piece, mixed
            )
        out_ref[rows, 0] = mixed.astype(BF).reshape(per, tok, width)


def attn_bwd_kernel(
    qkv_ref, grad_ref, doc_ref, cos_ref, sin_ref, out_ref, dk_ref, dv_ref, *, block_rows, tail
):
    parts, _, tok, width3 = qkv_ref.shape
    width = width3 // 3
    length = parts * tok
    heads = width // HEAD
    per = block_rows // tok
    k = qkv_ref[:, 0, :, width : 2 * width].reshape(length, width)
    v = qkv_ref[:, 0, :, 2 * width :].reshape(length, width)
    dk_ref[...] = jnp.zeros_like(dk_ref)
    dv_ref[...] = jnp.zeros_like(dv_ref)

    def unturn(values, place):
        return values * cos_ref[0, place, :] - half_swap(values) * sin_ref[0, place, :]

    for block in range(length // block_rows):
        rows = slice(block * per, (block + 1) * per)
        place = slice(block * block_rows, (block + 1) * block_rows)
        q = qkv_ref[rows, 0, :, :width].reshape(block_rows, width) * BF(score_scale)
        grad = grad_ref[rows, 0].reshape(block_rows, width)
        q_doc = doc_ref[0, place, :]
        q_pos = query_place(block, block_rows, length)
        segs = key_segments(block, block_rows, length, tail)
        allowed = [segment_allowed(s, q_pos, q_doc, length) for s in segs]
        dq = None
        for head in range(heads):
            q_h = jnp.where(head_mask(q.shape, head), q, BF(0)) if heads > 1 else q
            g_h = jnp.where(head_mask(grad.shape, head), grad, BF(0)) if heads > 1 else grad
            weights, inv = soft(masked_scores(q_h, k, segs, allowed))
            probs = [e * inv for e in weights]
            gp = [mm(g_h, v[a:b], NT) for a, b in segs]
            total = sum(jnp.sum(p * g, axis=1, keepdims=True) for p, g in zip(probs, gp))
            piece = None
            for (a, b), p, g in zip(segs, probs, gp):
                ds = (p * (g - total)).astype(BF)
                dv_ref[a:b, :] += mm(p.astype(BF), g_h, TN)
                dk_ref[a:b, :] += mm(ds, q_h, TN)
                part = mm(ds, k[a:b], NN)
                piece = part if piece is None else piece + part
            dq = piece if dq is None else jnp.where(head_mask(piece.shape, head), piece, dq)
        dq = unturn(dq * score_scale, place)
        out_ref[rows, 0, :, :width] = dq.astype(BF).reshape(per, tok, width)
    for block in range(length // block_rows):
        rows = slice(block * per, (block + 1) * per)
        place = slice(block * block_rows, (block + 1) * block_rows)
        dk = unturn(dk_ref[place, :], place)
        out_ref[rows, 0, :, width : 2 * width] = dk.astype(BF).reshape(per, tok, width)
        out_ref[rows, 0, :, 2 * width :] = (
            dv_ref[place, :].astype(BF).reshape(per, tok, width)
        )


def self_blocks(parts, tok):
    return max(tok, min(256, parts * tok)), min(128, tok)


def attend_self(qkv, doc_col):
    parts, seqs, tok, width3 = qkv.shape
    width = width3 // 3
    length = parts * tok
    block_rows, tail = self_blocks(parts, tok)
    pairs = seqs * (width // HEAD) * length * length
    return pl.pallas_call(
        functools.partial(attn_fwd_kernel, block_rows=block_rows, tail=tail),
        grid=(seqs,),
        in_specs=[
            pl.BlockSpec((parts, 1, tok, width3), lambda i: (0, i, 0, 0)),
            pl.BlockSpec((1, length, 1), lambda i: (i, 0, 0)),
        ],
        out_specs=pl.BlockSpec((parts, 1, tok, width), lambda i: (0, i, 0, 0)),
        out_shape=jax.ShapeDtypeStruct((parts, seqs, tok, width), BF),
        compiler_params=params(),
        cost_estimate=cost(pairs * 512, qkv.size * 3, pairs),
        name="attn_self_fwd",
    )(qkv, doc_col)


def attend_self_back(qkv, grad, doc_col, cos_all, sin_all):
    parts, seqs, tok, width3 = qkv.shape
    width = width3 // 3
    length = parts * tok
    block_rows, tail = self_blocks(parts, tok)
    pairs = seqs * (width // HEAD) * length * length
    rows_spec = pl.BlockSpec((1, length, width), lambda i: (i, 0, 0))
    return pl.pallas_call(
        functools.partial(attn_bwd_kernel, block_rows=block_rows, tail=tail),
        grid=(seqs,),
        in_specs=[
            pl.BlockSpec((parts, 1, tok, width3), lambda i: (0, i, 0, 0)),
            pl.BlockSpec((parts, 1, tok, width), lambda i: (0, i, 0, 0)),
            pl.BlockSpec((1, length, 1), lambda i: (i, 0, 0)),
            rows_spec,
            rows_spec,
        ],
        out_specs=pl.BlockSpec((parts, 1, tok, width3), lambda i: (0, i, 0, 0)),
        out_shape=jax.ShapeDtypeStruct(qkv.shape, BF),
        scratch_shapes=[pltpu.VMEM((length, width), F32), pltpu.VMEM((length, width), F32)],
        compiler_params=params(),
        cost_estimate=cost(pairs * 1280, qkv.size * 6, pairs),
        name="attn_self_bwd",
    )(qkv, grad, doc_col, cos_all, sin_all)


def cross_fwd_kernel(q_ref, k_ref, v_ref, valid_ref, out_ref):
    for pair in range(ATT // 128):
        lanes = slice(pair * 128, (pair + 1) * 128)
        q = q_ref[:, lanes] * BF(score_scale)
        k = k_ref[:, lanes]
        v = v_ref[:, lanes]
        mixed = None
        for head in range(2):
            q_h = jnp.where(head_mask(q.shape, head), q, BF(0))
            (weights,), inv = soft([mm(q_h, k, NT)])
            piece = mm((weights * inv).astype(BF), v, NN)
            mixed = piece if mixed is None else jnp.where(
                head_mask(piece.shape, head), piece, mixed
            )
        out_ref[:, lanes] = (mixed * valid_ref[...]).astype(BF)


def cross_bwd_kernel(q_ref, k_ref, v_ref, valid_ref, grad_ref, dq_ref, dkv_ref):
    for pair in range(ATT // 128):
        lanes = slice(pair * 128, (pair + 1) * 128)
        q = q_ref[:, lanes] * BF(score_scale)
        k = k_ref[:, lanes]
        v = v_ref[:, lanes]
        grad = (grad_ref[:, lanes].astype(F32) * valid_ref[...]).astype(BF)
        dq = dk = dv = None
        for head in range(2):
            q_h = jnp.where(head_mask(q.shape, head), q, BF(0))
            g_h = jnp.where(head_mask(grad.shape, head), grad, BF(0))
            (weights,), inv = soft([mm(q_h, k, NT)])
            probs = weights * inv
            gp = mm(g_h, v, NT)
            total = jnp.sum(probs * gp, axis=1, keepdims=True)
            ds = (probs * (gp - total)).astype(BF)
            part_v = mm(probs.astype(BF), g_h, TN)
            part_k = mm(ds, q_h, TN)
            part_q = mm(ds, k, NN)
            dv = part_v if dv is None else dv + part_v
            dk = part_k if dk is None else dk + part_k
            dq = part_q if dq is None else jnp.where(head_mask(part_q.shape, head), part_q, dq)
        dq_ref[:, lanes] = (dq * score_scale).astype(BF)
        dkv_ref[:, lanes] = dk.astype(BF)
        dkv_ref[:, ATT + pair * 128 : ATT + (pair + 1) * 128] = dv.astype(BF)


def cross_specs(rows, groups, retrieved):
    return [
        pl.BlockSpec((SPAN, ATT), lambda i: (i, 0)),
        pl.BlockSpec((retrieved, ATT), lambda i: (i, 0)),
        pl.BlockSpec((retrieved, ATT), lambda i: (i, 1)),
        pl.BlockSpec((SPAN, 1), lambda i: (i, 0)),
    ]


def attend_cross(query, kv, valid_col):
    rows = query.shape[0]
    groups = rows // SPAN
    retrieved = kv.shape[0] // groups
    return pl.pallas_call(
        cross_fwd_kernel,
        grid=(groups,),
        in_specs=cross_specs(rows, groups, retrieved),
        out_specs=pl.BlockSpec((SPAN, ATT), lambda i: (i, 0)),
        out_shape=jax.ShapeDtypeStruct(query.shape, BF),
        compiler_params=params(),
        cost_estimate=cost(rows * retrieved * ATT * 8, kv.size * 2 + query.size * 4),
        name="attn_cross_fwd",
    )(query, kv, kv, valid_col)


def attend_cross_back(query, kv, valid_col, grad):
    rows = query.shape[0]
    groups = rows // SPAN
    retrieved = kv.shape[0] // groups
    return pl.pallas_call(
        cross_bwd_kernel,
        grid=(groups,),
        in_specs=cross_specs(rows, groups, retrieved)
        + [pl.BlockSpec((SPAN, ATT), lambda i: (i, 0))],
        out_specs=[
            pl.BlockSpec((SPAN, ATT), lambda i: (i, 0)),
            pl.BlockSpec((retrieved, 2 * ATT), lambda i: (i, 0)),
        ],
        out_shape=[
            jax.ShapeDtypeStruct(query.shape, BF),
            jax.ShapeDtypeStruct(kv.shape, BF),
        ],
        compiler_params=params(),
        cost_estimate=cost(rows * retrieved * ATT * 20, kv.size * 4 + query.size * 6),
        name="attn_cross_bwd",
    )(query, kv, kv, valid_col, grad)


def ff_kernel(x_ref, cot_ref, win_ref, wdown_ref, late_ref, out_ref, gx_ref, gw_ref, acc_ref):
    step = pl.program_id(0)
    last = pl.num_programs(0) - 1
    model = x_ref.shape[1]
    x = x_ref[...]
    cot = cot_ref[...]
    u = mm(x, win_ref[...], NT)
    tangent = jnp.tanh(gelu_coef * (u + 0.044715 * u * u * u))
    act = (0.5 * u * (1.0 + tangent)).astype(BF)
    slope = 0.5 * (1.0 + tangent) + 0.5 * u * (1.0 - tangent * tangent) * gelu_coef * (
        1.0 + 3.0 * 0.044715 * u * u
    )
    gp = (mm(cot, wdown_ref[...], NT) * slope).astype(BF)
    gw_ref[:, :model] = mm(gp, x, TN).astype(BF)
    gw_ref[:, model:] = mm(act, cot, TN).astype(BF)
    out_part = mm(act, wdown_ref[...], NN)
    gx_part = mm(gp, win_ref[...], NN)

    @pl.when(step == 0)
    def _():
        acc_ref[...] = late_ref[...] + out_part
        gx_ref[...] = gx_part

    @pl.when(step > 0)
    def _():
        acc_ref[...] += out_part
        gx_ref[...] += gx_part

    @pl.when(step == last)
    def _():
        out_ref[...] = acc_ref[...].astype(BF)


def feed_forward(x, cot, ff_pair, late):
    rows, model = x.shape
    hidden = ff_pair.shape[0]
    block = hidden // 4
    full = lambda i: (0, 0)
    return pl.pallas_call(
        ff_kernel,
        grid=(hidden // block,),
        in_specs=[
            pl.BlockSpec((rows, model), full),
            pl.BlockSpec((rows, model), full),
            pl.BlockSpec((block, model), lambda i: (i, 0)),
            pl.BlockSpec((block, model), lambda i: (i, 1)),
            pl.BlockSpec((rows, model), full),
        ],
        out_specs=[
            pl.BlockSpec((rows, model), full),
            pl.BlockSpec((rows, model), full),
            pl.BlockSpec((block, 2 * model), lambda i: (i, 0)),
        ],
        out_shape=[
            jax.ShapeDtypeStruct((rows, model), BF),
            jax.ShapeDtypeStruct((rows, model), F32),
            jax.ShapeDtypeStruct((hidden, 2 * model), BF),
        ],
        scratch_shapes=[pltpu.VMEM((rows, model), F32)],
        compiler_params=params(),
        cost_estimate=cost(12 * rows * model * hidden, 8 * hidden * model, rows * hidden),
        name="feed_forward",
    )(x, cot, ff_pair, ff_pair, late)


def normalize(values):
    inv_rms = lax.rsqrt(jnp.mean(values * values, axis=-1, keepdims=True) + norm_eps)
    return values * inv_rms, inv_rms


def norm_back(grad_in, normed, inv_rms, gain):
    grad_normed = grad_in * gain
    grad_values = inv_rms * (
        grad_normed - normed * jnp.mean(grad_normed * normed, axis=-1, keepdims=True)
    )
    return grad_values, jnp.sum(grad_in * normed, axis=0)


def shift_in(values):
    count = lax.axis_size("seq")
    later = lax.ppermute(values[:, :SHIFT], "seq", [(i, (i - 1) % count) for i in range(count)])
    return jnp.concatenate([values[:, SHIFT:], later], axis=1)


def shift_out(values):
    count = lax.axis_size("seq")
    keep = values.shape[1] - SHIFT
    earlier = lax.ppermute(values[:, keep:], "seq", [(i, (i + 1) % count) for i in range(count)])
    return jnp.concatenate([earlier, values[:, :keep]], axis=1)


def total_over(values, axis):
    count = lax.axis_size(axis)
    if count & (count - 1):
        return lax.psum(values, axis)
    step = 1
    while step < count:
        values = values + lax.ppermute(values, axis, [(i, i ^ step) for i in range(count)])
        step *= 2
    return values


def on_device(tokens, doc_start, neighbours, qkv_w, out_w, ff_in, ff_out, gains, cotangent):
    parts = lax.axis_size("seq")
    seqs, tok, model = tokens.shape
    rows = seqs * tok
    length = parts * tok
    width = ATT // parts
    here = lax.axis_index("seq")

    qkv_t = lax.all_gather(qkv_w.T, BOTH, axis=0, tiled=True)
    out_t = lax.all_gather(out_w.T, BOTH, axis=0, tiled=True)
    ff_pair = lax.all_gather(
        jnp.concatenate([ff_in.T, ff_out], axis=1), BOTH, axis=0, tiled=True
    )

    doc_all = lax.all_gather(doc_start, "seq", axis=1, tiled=True)
    doc_all = jnp.roll(doc_all, -SHIFT, axis=1)
    place_all = (jnp.arange(length, dtype=jnp.int32) + SHIFT) % length
    frequency = jnp.exp(
        (jnp.arange(width) % (HEAD // 2)).astype(F32) * (-math.log(10000.0) / (HEAD // 2))
    )
    sign = jnp.where(jnp.arange(width) % HEAD < HEAD // 2, -1.0, 1.0).astype(F32)
    angles = (place_all[None] - doc_all).astype(F32)[..., None] * frequency
    cos_all = jnp.cos(angles)
    sin_all = jnp.sin(angles) * sign
    local = lambda table: lax.dynamic_slice_in_dim(table, here * tok, tok, axis=1)
    cos_rows = local(cos_all).reshape(rows, width)
    sin_rows = local(sin_all).reshape(rows, width)
    doc_rows = local(doc_all)
    place = lax.dynamic_slice_in_dim(place_all, here * tok, tok, axis=0)
    doc_col = doc_all[..., None]
    span_of = (place + 1) // SPAN - 1
    valid_col = (
        ((span_of[None] >= 0) & (doc_rows <= span_of[None] * SPAN + SPAN - 1))
        .astype(F32)
        .reshape(rows, 1)
    )

    resid_in = shift_in(tokens).reshape(rows, model).astype(F32)
    cot = shift_in(cotangent).reshape(rows, model)
    nb = neighbours.reshape(-1, model)

    norm_one, inv_one = normalize(resid_in)
    input_one = (norm_one * gains[0]).astype(BF)
    qkv_mine = project_self(input_one, qkv_t, cos_rows, sin_rows, parts)
    qkv_heads = lax.all_to_all(qkv_mine, "seq", 0, 0).reshape(parts, seqs, tok, 3 * width)
    kv = mm(nb, qkv_t[4 * ATT :], NT).astype(BF)
    mixed = attend_self(qkv_heads, doc_col).reshape(parts, rows, width)
    attn_self = lax.all_to_all(mixed, "seq", 0, 0).transpose(1, 0, 2).reshape(rows, ATT)
    resid_mid = resid_in + mm(attn_self, out_t[:model], NT)
    norm_two, inv_two = normalize(resid_mid)
    input_two = (norm_two * gains[1]).astype(BF)
    query_cross = mm(input_two, qkv_t[3 * ATT : 4 * ATT], NT).astype(BF)
    attn_cross = attend_cross(query_cross, kv, valid_col)
    resid_late = resid_mid + mm(attn_cross, out_t[model:], NT)
    norm_three, inv_three = normalize(resid_late)
    input_three = (norm_three * gains[2]).astype(BF)

    output, grad_three, grad_ff = feed_forward(input_three, cot, ff_pair, resid_late)
    shard_ff = lax.psum_scatter(grad_ff, BOTH, scatter_dimension=0, tiled=True)

    back_three, gain_three = norm_back(grad_three, norm_three, inv_three, gains[2])
    grad_late = cot.astype(F32) + back_three
    grad_two = grad_late.astype(BF)
    grad_out_cross = mm(grad_two, attn_cross, TN).astype(BF)
    grad_cross_out = mm(grad_two, out_t[model:], NN).astype(BF)
    grad_query, grad_kv = attend_cross_back(query_cross, kv, valid_col, grad_cross_out)
    grad_neighbours = mm(grad_kv, qkv_t[4 * ATT :], NN)
    grad_w_kv = mm(grad_kv, nb, TN).astype(BF)
    grad_w_q = mm(grad_query, input_two, TN).astype(BF)
    back_two, gain_two = norm_back(
        mm(grad_query, qkv_t[3 * ATT : 4 * ATT], NN), norm_two, inv_two, gains[1]
    )
    grad_mid = grad_late + back_two
    grad_one = grad_mid.astype(BF)
    grad_out_self = mm(grad_one, attn_self, TN).astype(BF)
    grad_attn = mm(grad_one, out_t[:model], NN).astype(BF)
    grad_attn = grad_attn.reshape(rows, parts, width).transpose(1, 0, 2)
    grad_heads = lax.all_to_all(grad_attn, "seq", 0, 0).reshape(parts, seqs, tok, width)
    shard_out = lax.psum_scatter(
        jnp.concatenate([grad_out_self, grad_out_cross], axis=0),
        BOTH,
        scatter_dimension=0,
        tiled=True,
    )
    grad_qkv_heads = attend_self_back(qkv_heads, grad_heads, doc_col, cos_all, sin_all)
    grad_lin = lax.all_to_all(grad_qkv_heads.reshape(parts, rows, 3 * width), "seq", 0, 0)
    grad_lin = grad_lin.reshape(parts, rows, 3, width).transpose(1, 2, 0, 3).reshape(rows, 3 * ATT)
    grad_w_self = mm(grad_lin, input_one, TN).astype(BF)
    shard_qkv = lax.psum_scatter(
        jnp.concatenate([grad_w_self, grad_w_q, grad_w_kv], axis=0),
        BOTH,
        scatter_dimension=0,
        tiled=True,
    )
    back_one, gain_one = norm_back(mm(grad_lin, qkv_t[: 3 * ATT], NN), norm_one, inv_one, gains[0])
    grad_tokens = shift_out((grad_mid + back_one).reshape(seqs, tok, model))
    grad_gains = total_over(
        total_over(jnp.stack([gain_one, gain_two, gain_three]), "seq"), "batch"
    )

    shard_ff = shard_ff.astype(F32)
    return (
        shift_out(output.reshape(seqs, tok, model)),
        grad_tokens,
        grad_neighbours.reshape(neighbours.shape),
        shard_qkv.astype(F32).T,
        shard_out.astype(F32).T,
        shard_ff[:, :model].T,
        shard_ff[:, model:],
        grad_gains,
    )


def solution(mesh):
    rows = P("batch", "seq", None)
    by_column = P(None, BOTH)
    return jax.shard_map(
        on_device,
        mesh=mesh,
        in_specs=(
            rows,
            P("batch", "seq"),
            P("batch", "seq", None, None),
            by_column,
            by_column,
            by_column,
            P(BOTH, None),
            P(),
            rows,
        ),
        out_specs=(
            rows,
            rows,
            P("batch", "seq", None, None),
            by_column,
            by_column,
            by_column,
            P(BOTH, None),
            P(),
        ),
        check_vma=False,
    )
```

```python
import functools
import math

import jax
import jax.numpy as jnp
from jax import lax
from jax.experimental import pallas as pl
from jax.experimental.pallas import tpu as pltpu
from jax.sharding import PartitionSpec as P

HEADS = 16
HEAD = 64
SPAN = 64
ATT = HEADS * HEAD
SHIFT = SPAN - 1
BOTH = ("seq", "batch")

score_scale = 0.125
gelu_coef = math.sqrt(2.0 / math.pi)
norm_eps = 1e-05
BF = jnp.bfloat16
F32 = jnp.float32

NT = (((1,), (1,)), ((), ()))
NN = (((1,), (0,)), ((), ()))
TN = (((0,), (0,)), ((), ()))


def mm(left, right, dims):
    return lax.dot_general(left, right, dims, preferred_element_type=F32)


def params(**kw):
    return pltpu.CompilerParams(vmem_limit_bytes=60 * 1024 * 1024, **kw)


def cost(flops, size, exps=0):
    return pl.CostEstimate(flops=int(flops), bytes_accessed=int(size), transcendentals=int(exps))


def half_swap(values):
    width = values.shape[-1]
    half = HEAD // 2
    lane = lax.broadcasted_iota(jnp.int32, values.shape, 1)
    if width % 128 == 0:
        ahead = pltpu.roll(values, width - half, 1)
        behind = pltpu.roll(values, half, 1)
    else:
        ahead = jnp.concatenate([values[:, half:], values[:, :half]], axis=1)
        behind = jnp.concatenate([values[:, -half:], values[:, :-half]], axis=1)
    return jnp.where(lane % HEAD < half, ahead, behind)


def proj_kernel(x_ref, wq_ref, wk_ref, wv_ref, cos_ref, sin_ref, out_ref):
    groups, _, width3 = out_ref.shape
    width = width3 // 3
    x = x_ref[...]
    for part, w_ref in enumerate((wq_ref, wk_ref, wv_ref)):
        acc = mm(x, w_ref[...], NT)
        for g in range(groups):
            piece = acc[:, g * width : (g + 1) * width]
            if part < 2:
                piece = piece * cos_ref[...] + half_swap(piece) * sin_ref[...]
            out_ref[g, :, part * width : (part + 1) * width] = piece.astype(BF)


def project_self(x, qkv_t, cos_rows, sin_rows, parts):
    rows, model = x.shape
    width = ATT // parts
    groups = 2 if width % 128 == 0 else 1
    steps = parts // groups
    wide = groups * width
    full = lambda i: (0, 0)
    return pl.pallas_call(
        proj_kernel,
        grid=(steps,),
        in_specs=[
            pl.BlockSpec((rows, model), full),
            pl.BlockSpec((wide, model), lambda i: (i, 0)),
            pl.BlockSpec((wide, model), lambda i: (steps + i, 0)),
            pl.BlockSpec((wide, model), lambda i: (2 * steps + i, 0)),
            pl.BlockSpec((rows, width), full),
            pl.BlockSpec((rows, width), full),
        ],
        out_specs=pl.BlockSpec((groups, rows, 3 * width), lambda i: (i, 0, 0)),
        out_shape=jax.ShapeDtypeStruct((parts, rows, 3 * width), BF),
        compiler_params=params(),
        cost_estimate=cost(2 * rows * model * 3 * ATT, 2 * (3 * ATT * model + rows * 4 * ATT)),
        name="proj_self",
    )(x, qkv_t, qkv_t, qkv_t, cos_rows, sin_rows)


def head_mask(shape, head):
    lane = lax.broadcasted_iota(jnp.int32, shape, 1)
    return lane // HEAD == head


def key_segments(block, block_rows, length, tail):
    stop = (block + 1) * block_rows
    if stop + tail > length:
        return [(0, length)]
    return [(0, stop), (length - tail, length)]


def segment_allowed(segment, q_pos, q_doc, length):
    start, stop = segment
    index = lax.broadcasted_iota(jnp.int32, (1, stop - start), 1) + start
    k_pos = jnp.where(index + SHIFT >= length, index + SHIFT - length, index + SHIFT)
    return (k_pos >= q_doc) & (k_pos <= q_pos)


def query_place(block, block_rows, length):
    index = lax.broadcasted_iota(jnp.int32, (block_rows, 1), 0) + block * block_rows
    return jnp.where(index + SHIFT >= length, index + SHIFT - length, index + SHIFT)


def masked_scores(q_h, k, segs, allowed):
    return [
        jnp.where(ok, mm(q_h, k[a:b], NT), -1e30) for (a, b), ok in zip(segs, allowed)
    ]


def soft(scores):
    top = functools.reduce(jnp.maximum, [jnp.max(s, axis=1, keepdims=True) for s in scores])
    weights = [jnp.exp(s - top) for s in scores]
    total = sum(jnp.sum(e, axis=1, keepdims=True) for e in weights)
    return weights, 1.0 / total


def attn_fwd_kernel(qkv_ref, doc_ref, out_ref, *, block_rows, tail):
    parts, _, tok, width3 = qkv_ref.shape
    width = width3 // 3
    length = parts * tok
    heads = width // HEAD
    per = block_rows // tok
    k = qkv_ref[:, 0, :, width : 2 * width].reshape(length, width)
    v = qkv_ref[:, 0, :, 2 * width :].reshape(length, width)
    for block in range(length // block_rows):
        rows = slice(block * per, (block + 1) * per)
        q = qkv_ref[rows, 0, :, :width].reshape(block_rows, width) * BF(score_scale)
        q_doc = doc_ref[0, block * block_rows : (block + 1) * block_rows, :]
        q_pos = query_place(block, block_rows, length)
        segs = key_segments(block, block_rows, length, tail)
        allowed = [segment_allowed(s, q_pos, q_doc, length) for s in segs]
        mixed = None
        for head in range(heads):
            q_h = jnp.where(head_mask(q.shape, head), q, BF(0)) if heads > 1 else q
            weights, inv = soft(masked_scores(q_h, k, segs, allowed))
            piece = sum(mm(e.astype(BF), v[a:b], NN) for e, (a, b) in zip(weights, segs)) * inv
            mixed = piece if mixed is None else jnp.where(
                head_mask(piece.shape, head), piece, mixed
            )
        out_ref[rows, 0] = mixed.astype(BF).reshape(per, tok, width)


def attn_bwd_kernel(
    qkv_ref, grad_ref, doc_ref, cos_ref, sin_ref, out_ref, dk_ref, dv_ref, *, block_rows, tail
):
    parts, _, tok, width3 = qkv_ref.shape
    width = width3 // 3
    length = parts * tok
    heads = width // HEAD
    per = block_rows // tok
    k = qkv_ref[:, 0, :, width : 2 * width].reshape(length, width)
    v = qkv_ref[:, 0, :, 2 * width :].reshape(length, width)
    dk_ref[...] = jnp.zeros_like(dk_ref)
    dv_ref[...] = jnp.zeros_like(dv_ref)

    def unturn(values, place):
        return values * cos_ref[0, place, :] - half_swap(values) * sin_ref[0, place, :]

    for block in range(length // block_rows):
        rows = slice(block * per, (block + 1) * per)
        place = slice(block * block_rows, (block + 1) * block_rows)
        q = qkv_ref[rows, 0, :, :width].reshape(block_rows, width) * BF(score_scale)
        grad = grad_ref[rows, 0].reshape(block_rows, width)
        q_doc = doc_ref[0, place, :]
        q_pos = query_place(block, block_rows, length)
        segs = key_segments(block, block_rows, length, tail)
        allowed = [segment_allowed(s, q_pos, q_doc, length) for s in segs]
        dq = None
        for head in range(heads):
            q_h = jnp.where(head_mask(q.shape, head), q, BF(0)) if heads > 1 else q
            g_h = jnp.where(head_mask(grad.shape, head), grad, BF(0)) if heads > 1 else grad
            weights, inv = soft(masked_scores(q_h, k, segs, allowed))
            probs = [e * inv for e in weights]
            gp = [mm(g_h, v[a:b], NT) for a, b in segs]
            total = sum(jnp.sum(p * g, axis=1, keepdims=True) for p, g in zip(probs, gp))
            piece = None
            for (a, b), p, g in zip(segs, probs, gp):
                ds = (p * (g - total)).astype(BF)
                dv_ref[a:b, :] += mm(p.astype(BF), g_h, TN)
                dk_ref[a:b, :] += mm(ds, q_h, TN)
                part = mm(ds, k[a:b], NN)
                piece = part if piece is None else piece + part
            dq = piece if dq is None else jnp.where(head_mask(piece.shape, head), piece, dq)
        dq = unturn(dq * score_scale, place)
        out_ref[rows, 0, :, :width] = dq.astype(BF).reshape(per, tok, width)
    for block in range(length // block_rows):
        rows = slice(block * per, (block + 1) * per)
        place = slice(block * block_rows, (block + 1) * block_rows)
        dk = unturn(dk_ref[place, :], place)
        out_ref[rows, 0, :, width : 2 * width] = dk.astype(BF).reshape(per, tok, width)
        out_ref[rows, 0, :, 2 * width :] = (
            dv_ref[place, :].astype(BF).reshape(per, tok, width)
        )


def self_blocks(parts, tok):
    return max(tok, min(256, parts * tok)), min(128, tok)


def attend_self(qkv, doc_col):
    parts, seqs, tok, width3 = qkv.shape
    width = width3 // 3
    length = parts * tok
    block_rows, tail = self_blocks(parts, tok)
    pairs = seqs * (width // HEAD) * length * length
    return pl.pallas_call(
        functools.partial(attn_fwd_kernel, block_rows=block_rows, tail=tail),
        grid=(seqs,),
        in_specs=[
            pl.BlockSpec((parts, 1, tok, width3), lambda i: (0, i, 0, 0)),
            pl.BlockSpec((1, length, 1), lambda i: (i, 0, 0)),
        ],
        out_specs=pl.BlockSpec((parts, 1, tok, width), lambda i: (0, i, 0, 0)),
        out_shape=jax.ShapeDtypeStruct((parts, seqs, tok, width), BF),
        compiler_params=params(),
        cost_estimate=cost(pairs * 512, qkv.size * 3, pairs),
        name="attn_self_fwd",
    )(qkv, doc_col)


def attend_self_back(qkv, grad, doc_col, cos_all, sin_all):
    parts, seqs, tok, width3 = qkv.shape
    width = width3 // 3
    length = parts * tok
    block_rows, tail = self_blocks(parts, tok)
    pairs = seqs * (width // HEAD) * length * length
    rows_spec = pl.BlockSpec((1, length, width), lambda i: (i, 0, 0))
    return pl.pallas_call(
        functools.partial(attn_bwd_kernel, block_rows=block_rows, tail=tail),
        grid=(seqs,),
        in_specs=[
            pl.BlockSpec((parts, 1, tok, width3), lambda i: (0, i, 0, 0)),
            pl.BlockSpec((parts, 1, tok, width), lambda i: (0, i, 0, 0)),
            pl.BlockSpec((1, length, 1), lambda i: (i, 0, 0)),
            rows_spec,
            rows_spec,
        ],
        out_specs=pl.BlockSpec((parts, 1, tok, width3), lambda i: (0, i, 0, 0)),
        out_shape=jax.ShapeDtypeStruct(qkv.shape, BF),
        scratch_shapes=[pltpu.VMEM((length, width), F32), pltpu.VMEM((length, width), F32)],
        compiler_params=params(),
        cost_estimate=cost(pairs * 1280, qkv.size * 6, pairs),
        name="attn_self_bwd",
    )(qkv, grad, doc_col, cos_all, sin_all)


def cross_fwd_kernel(q_ref, k_ref, v_ref, valid_ref, out_ref):
    for pair in range(ATT // 128):
        lanes = slice(pair * 128, (pair + 1) * 128)
        q = q_ref[:, lanes] * BF(score_scale)
        k = k_ref[:, lanes]
        v = v_ref[:, lanes]
        mixed = None
        for head in range(2):
            q_h = jnp.where(head_mask(q.shape, head), q, BF(0))
            (weights,), inv = soft([mm(q_h, k, NT)])
            piece = mm((weights * inv).astype(BF), v, NN)
            mixed = piece if mixed is None else jnp.where(
                head_mask(piece.shape, head), piece, mixed
            )
        out_ref[:, lanes] = (mixed * valid_ref[...]).astype(BF)


def cross_bwd_kernel(q_ref, k_ref, v_ref, valid_ref, grad_ref, dq_ref, dkv_ref):
    for pair in range(ATT // 128):
        lanes = slice(pair * 128, (pair + 1) * 128)
        q = q_ref[:, lanes] * BF(score_scale)
        k = k_ref[:, lanes]
        v = v_ref[:, lanes]
        grad = (grad_ref[:, lanes].astype(F32) * valid_ref[...]).astype(BF)
        dq = dk = dv = None
        for head in range(2):
            q_h = jnp.where(head_mask(q.shape, head), q, BF(0))
            g_h = jnp.where(head_mask(grad.shape, head), grad, BF(0))
            (weights,), inv = soft([mm(q_h, k, NT)])
            probs = weights * inv
            gp = mm(g_h, v, NT)
            total = jnp.sum(probs * gp, axis=1, keepdims=True)
            ds = (probs * (gp - total)).astype(BF)
            part_v = mm(probs.astype(BF), g_h, TN)
            part_k = mm(ds, q_h, TN)
            part_q = mm(ds, k, NN)
            dv = part_v if dv is None else dv + part_v
            dk = part_k if dk is None else dk + part_k
            dq = part_q if dq is None else jnp.where(head_mask(part_q.shape, head), part_q, dq)
        dq_ref[:, lanes] = (dq * score_scale).astype(BF)
        dkv_ref[:, lanes] = dk.astype(BF)
        dkv_ref[:, ATT + pair * 128 : ATT + (pair + 1) * 128] = dv.astype(BF)


def cross_specs(rows, groups, retrieved):
    return [
        pl.BlockSpec((SPAN, ATT), lambda i: (i, 0)),
        pl.BlockSpec((retrieved, ATT), lambda i: (i, 0)),
        pl.BlockSpec((retrieved, ATT), lambda i: (i, 1)),
        pl.BlockSpec((SPAN, 1), lambda i: (i, 0)),
    ]


def attend_cross(query, kv, valid_col):
    rows = query.shape[0]
    groups = rows // SPAN
    retrieved = kv.shape[0] // groups
    return pl.pallas_call(
        cross_fwd_kernel,
        grid=(groups,),
        in_specs=cross_specs(rows, groups, retrieved),
        out_specs=pl.BlockSpec((SPAN, ATT), lambda i: (i, 0)),
        out_shape=jax.ShapeDtypeStruct(query.shape, BF),
        compiler_params=params(),
        cost_estimate=cost(rows * retrieved * ATT * 8, kv.size * 2 + query.size * 4),
        name="attn_cross_fwd",
    )(query, kv, kv, valid_col)


def attend_cross_back(query, kv, valid_col, grad):
    rows = query.shape[0]
    groups = rows // SPAN
    retrieved = kv.shape[0] // groups
    return pl.pallas_call(
        cross_bwd_kernel,
        grid=(groups,),
        in_specs=cross_specs(rows, groups, retrieved)
        + [pl.BlockSpec((SPAN, ATT), lambda i: (i, 0))],
        out_specs=[
            pl.BlockSpec((SPAN, ATT), lambda i: (i, 0)),
            pl.BlockSpec((retrieved, 2 * ATT), lambda i: (i, 0)),
        ],
        out_shape=[
            jax.ShapeDtypeStruct(query.shape, BF),
            jax.ShapeDtypeStruct(kv.shape, BF),
        ],
        compiler_params=params(),
        cost_estimate=cost(rows * retrieved * ATT * 20, kv.size * 4 + query.size * 6),
        name="attn_cross_bwd",
    )(query, kv, kv, valid_col, grad)


def ff_kernel(x_ref, cot_ref, win_ref, wdown_ref, late_ref, out_ref, gx_ref, gw_ref, acc_ref):
    step = pl.program_id(0)
    last = pl.num_programs(0) - 1
    model = x_ref.shape[1]
    x = x_ref[...]
    cot = cot_ref[...]
    u = mm(x, win_ref[...], NT)
    tangent = jnp.tanh(gelu_coef * (u + 0.044715 * u * u * u))
    act = (0.5 * u * (1.0 + tangent)).astype(BF)
    slope = 0.5 * (1.0 + tangent) + 0.5 * u * (1.0 - tangent * tangent) * gelu_coef * (
        1.0 + 3.0 * 0.044715 * u * u
    )
    gp = (mm(cot, wdown_ref[...], NT) * slope).astype(BF)
    gw_ref[:, :model] = mm(gp, x, TN).astype(BF)
    gw_ref[:, model:] = mm(act, cot, TN).astype(BF)
    out_part = mm(act, wdown_ref[...], NN)
    gx_part = mm(gp, win_ref[...], NN)

    @pl.when(step == 0)
    def _():
        acc_ref[...] = late_ref[...] + out_part
        gx_ref[...] = gx_part

    @pl.when(step > 0)
    def _():
        acc_ref[...] += out_part
        gx_ref[...] += gx_part

    @pl.when(step == last)
    def _():
        out_ref[...] = acc_ref[...].astype(BF)


def feed_forward(x, cot, ff_pair, late):
    rows, model = x.shape
    hidden = ff_pair.shape[0]
    block = hidden // 4
    full = lambda i: (0, 0)
    return pl.pallas_call(
        ff_kernel,
        grid=(hidden // block,),
        in_specs=[
            pl.BlockSpec((rows, model), full),
            pl.BlockSpec((rows, model), full),
            pl.BlockSpec((block, model), lambda i: (i, 0)),
            pl.BlockSpec((block, model), lambda i: (i, 1)),
            pl.BlockSpec((rows, model), full),
        ],
        out_specs=[
            pl.BlockSpec((rows, model), full),
            pl.BlockSpec((rows, model), full),
            pl.BlockSpec((block, 2 * model), lambda i: (i, 0)),
        ],
        out_shape=[
            jax.ShapeDtypeStruct((rows, model), BF),
            jax.ShapeDtypeStruct((rows, model), F32),
            jax.ShapeDtypeStruct((hidden, 2 * model), BF),
        ],
        scratch_shapes=[pltpu.VMEM((rows, model), F32)],
        compiler_params=params(),
        cost_estimate=cost(12 * rows * model * hidden, 8 * hidden * model, rows * hidden),
        name="feed_forward",
    )(x, cot, ff_pair, ff_pair, late)


def normalize(values):
    inv_rms = lax.rsqrt(jnp.mean(values * values, axis=-1, keepdims=True) + norm_eps)
    return values * inv_rms, inv_rms


def norm_back(grad_in, normed, inv_rms, gain):
    grad_normed = grad_in * gain
    grad_values = inv_rms * (
        grad_normed - normed * jnp.mean(grad_normed * normed, axis=-1, keepdims=True)
    )
    return grad_values, jnp.sum(grad_in * normed, axis=0)


def shift_in(values):
    count = lax.axis_size("seq")
    later = lax.ppermute(values[:, :SHIFT], "seq", [(i, (i - 1) % count) for i in range(count)])
    return jnp.concatenate([values[:, SHIFT:], later], axis=1)


def shift_out(values):
    count = lax.axis_size("seq")
    keep = values.shape[1] - SHIFT
    earlier = lax.ppermute(values[:, keep:], "seq", [(i, (i + 1) % count) for i in range(count)])
    return jnp.concatenate([earlier, values[:, :keep]], axis=1)


def paired(values, axis, stride):
    count = lax.axis_size(axis)
    return lax.ppermute(values, axis, [(i, i ^ stride) for i in range(count)])


def bit_of(axis, stride):
    return (lax.axis_index(axis) // stride) % 2


def bits_of(axis):
    count = lax.axis_size(axis)
    return [(axis, 1 << k) for k in range(count.bit_length() - 1)]


def index_bits():
    bits = bits_of("seq")[:-1][::-1] + bits_of("batch")[::-1]
    return {bit: dim for dim, bit in enumerate(bits)}


def top_bit():
    return bits_of("seq")[-1]


def stage_orders():
    core, *across = bits_of("batch")
    low, *along = bits_of("seq")[:-1]
    return core, (across + [low], [low] + across), along


def total_over(values, axis):
    for bit in bits_of(axis):
        values = values + paired(values, *bit)
    return values


def grown(values, bit, dim):
    other = paired(values, *bit)
    both = jnp.stack([other, other], axis=dim)
    return lax.dynamic_update_index_in_dim(both, values, bit_of(*bit), dim)


def pick(values, index, dim):
    return lax.dynamic_index_in_dim(values, index, dim, keepdims=False)


def halved(values, bit, dim):
    mine = bit_of(*bit)
    other = paired(pick(values, 1 - mine, dim), *bit)
    return (pick(values, mine, dim).astype(F32) + other.astype(F32)).astype(BF)


def gather_half(piece, split):
    dims = index_bits()
    core, orders, along = stage_orders()
    held = []

    def grow(values, bit):
        dim = sum(dims[b] < dims[bit] for b in held)
        held.append(bit)
        return grown(values, bit, dim)

    for bit in along[::-1]:
        piece = grow(piece, bit)
    base = list(held)
    colors = []
    for part, order in zip(jnp.split(piece, 2, axis=piece.ndim - 2 + split), orders):
        held[:] = base
        for bit in order[::-1]:
            part = grow(part, bit)
        colors.append(part)
    last = len(dims) - 1
    shape = list(colors[0].shape)
    shape.insert(last, 2)
    shape.insert(last + 1 + split, 2)
    whole = jnp.zeros(shape, colors[0].dtype)
    mine = bit_of(*core)
    for k, part in enumerate(colors):
        for slot, values in ((mine, part), (1 - mine, paired(part, *core))):
            block = jnp.expand_dims(jnp.expand_dims(values, last), last + 1 + split)
            start = [0] * len(shape)
            start[last] = slot
            start[last + 1 + split] = k
            whole = lax.dynamic_update_slice(whole, block, start)
    columns = shape[-1] * (2 if split else 1)
    return whole.reshape(-1, columns)


def scatter_half(grads, rows, split, owner):
    dims = index_bits()
    core, orders, along = stage_orders()
    columns = grads.shape[1]
    grid = grads.reshape([2] * len(dims) + [rows, columns])
    results = []
    for k, order in enumerate(orders):
        part = lax.slice_in_dim(
            grid,
            k * grid.shape[len(dims) + split] // 2,
            (k + 1) * grid.shape[len(dims) + split] // 2,
            axis=len(dims) + split,
        )
        left = dict(dims)
        for bit in [core] + order + along:
            dim = sum(left[b] < left[bit] for b in left)
            part = halved(part, bit, dim)
            del left[bit]
        axis, stride = top_bit()
        count = lax.axis_size(axis)
        senders = [i for i in range(count) if (i // stride) % 2 != owner]
        other = lax.ppermute(part, axis, [(i, i ^ stride) for i in senders])
        results.append(part.astype(F32) + other.astype(F32))
    return jnp.concatenate(results, axis=split)


def on_device(tokens, doc_start, neighbours, qkv_w, out_w, ff_in, ff_out, gains, cotangent):
    parts = lax.axis_size("seq")
    seqs, tok, model = tokens.shape
    rows = seqs * tok
    length = parts * tok
    width = ATT // parts
    here = lax.axis_index("seq")

    upper = bit_of(*top_bit()) == 1
    qkv_own = qkv_w.T
    qkv_other = paired(qkv_own, *top_bit())
    w_self = gather_half(jnp.where(upper, qkv_other, qkv_own), 0)
    w_cross = gather_half(jnp.where(upper, qkv_own, qkv_other), 0)
    w_q, w_kv = w_cross[:ATT], w_cross[ATT:]
    out_t = lax.all_gather(out_w.T, BOTH, axis=0, tiled=True)
    ff_pair = lax.all_gather(
        jnp.concatenate([ff_in.T, ff_out], axis=1), BOTH, axis=0, tiled=True
    )

    doc_all = doc_start[None]
    for bit in bits_of("seq"):
        doc_all = grown(doc_all, bit, 0).reshape(-1, seqs, tok)
    doc_all = jnp.roll(doc_all.transpose(1, 0, 2).reshape(seqs, length), -SHIFT, axis=1)
    place_all = (jnp.arange(length, dtype=jnp.int32) + SHIFT) % length
    frequency = jnp.exp(
        (jnp.arange(width) % (HEAD // 2)).astype(F32) * (-math.log(10000.0) / (HEAD // 2))
    )
    sign = jnp.where(jnp.arange(width) % HEAD < HEAD // 2, -1.0, 1.0).astype(F32)
    angles = (place_all[None] - doc_all).astype(F32)[..., None] * frequency
    cos_all = jnp.cos(angles)
    sin_all = jnp.sin(angles) * sign
    local = lambda table: lax.dynamic_slice_in_dim(table, here * tok, tok, axis=1)
    cos_rows = local(cos_all).reshape(rows, width)
    sin_rows = local(sin_all).reshape(rows, width)
    doc_rows = local(doc_all)
    place = lax.dynamic_slice_in_dim(place_all, here * tok, tok, axis=0)
    doc_col = doc_all[..., None]
    span_of = (place + 1) // SPAN - 1
    valid_col = (
        ((span_of[None] >= 0) & (doc_rows <= span_of[None] * SPAN + SPAN - 1))
        .astype(F32)
        .reshape(rows, 1)
    )

    resid_in = shift_in(tokens).reshape(rows, model).astype(F32)
    cot = shift_in(cotangent).reshape(rows, model)
    nb = neighbours.reshape(-1, model)

    norm_one, inv_one = normalize(resid_in)
    input_one = (norm_one * gains[0]).astype(BF)
    qkv_mine = project_self(input_one, w_self, cos_rows, sin_rows, parts)
    qkv_heads = lax.all_to_all(qkv_mine, "seq", 0, 0).reshape(parts, seqs, tok, 3 * width)
    kv = mm(nb, w_kv, NT).astype(BF)
    mixed = attend_self(qkv_heads, doc_col).reshape(parts, rows, width)
    attn_self = lax.all_to_all(mixed, "seq", 0, 0).transpose(1, 0, 2).reshape(rows, ATT)
    resid_mid = resid_in + mm(attn_self, out_t[:model], NT)
    norm_two, inv_two = normalize(resid_mid)
    input_two = (norm_two * gains[1]).astype(BF)
    query_cross = mm(input_two, w_q, NT).astype(BF)
    attn_cross = attend_cross(query_cross, kv, valid_col)
    resid_late = resid_mid + mm(attn_cross, out_t[model:], NT)
    norm_three, inv_three = normalize(resid_late)
    input_three = (norm_three * gains[2]).astype(BF)

    output, grad_three, grad_ff = feed_forward(input_three, cot, ff_pair, resid_late)
    shard_ff = lax.psum_scatter(grad_ff, BOTH, scatter_dimension=0, tiled=True)

    back_three, gain_three = norm_back(grad_three, norm_three, inv_three, gains[2])
    grad_late = cot.astype(F32) + back_three
    grad_two = grad_late.astype(BF)
    grad_out_cross = mm(grad_two, attn_cross, TN).astype(BF)
    grad_cross_out = mm(grad_two, out_t[model:], NN).astype(BF)
    grad_query, grad_kv = attend_cross_back(query_cross, kv, valid_col, grad_cross_out)
    grad_neighbours = mm(grad_kv, w_kv, NN)
    grad_w_kv = mm(grad_kv, nb, TN).astype(BF)
    grad_w_q = mm(grad_query, input_two, TN).astype(BF)
    back_two, gain_two = norm_back(
        mm(grad_query, w_q, NN), norm_two, inv_two, gains[1]
    )
    grad_mid = grad_late + back_two
    grad_one = grad_mid.astype(BF)
    grad_out_self = mm(grad_one, attn_self, TN).astype(BF)
    grad_attn = mm(grad_one, out_t[:model], NN).astype(BF)
    grad_attn = grad_attn.reshape(rows, parts, width).transpose(1, 0, 2)
    grad_heads = lax.all_to_all(grad_attn, "seq", 0, 0).reshape(parts, seqs, tok, width)
    out_rows = 2 * model // (parts * lax.axis_size("batch"))
    qkv_rows = 6 * ATT // (parts * lax.axis_size("batch"))
    shard_out = jnp.where(
        upper,
        scatter_half(grad_out_cross, out_rows, 1, 1),
        scatter_half(grad_out_self, out_rows, 1, 0),
    )
    grad_qkv_heads = attend_self_back(qkv_heads, grad_heads, doc_col, cos_all, sin_all)
    grad_lin = lax.all_to_all(grad_qkv_heads.reshape(parts, rows, 3 * width), "seq", 0, 0)
    grad_lin = grad_lin.reshape(parts, rows, 3, width).transpose(1, 2, 0, 3).reshape(rows, 3 * ATT)
    grad_w_self = mm(grad_lin, input_one, TN).astype(BF)
    shard_qkv = jnp.where(
        upper,
        scatter_half(jnp.concatenate([grad_w_q, grad_w_kv], axis=0), qkv_rows, 0, 1),
        scatter_half(grad_w_self, qkv_rows, 0, 0),
    )
    back_one, gain_one = norm_back(mm(grad_lin, w_self, NN), norm_one, inv_one, gains[0])
    grad_tokens = shift_out((grad_mid + back_one).reshape(seqs, tok, model))
    grad_gains = total_over(
        total_over(jnp.stack([gain_one, gain_two, gain_three]), "seq"), "batch"
    )

    shard_ff = shard_ff.astype(F32)
    return (
        shift_out(output.reshape(seqs, tok, model)),
        grad_tokens,
        grad_neighbours.reshape(neighbours.shape),
        shard_qkv.T,
        shard_out.T,
        shard_ff[:, :model].T,
        shard_ff[:, model:],
        grad_gains,
    )


def solution(mesh):
    rows = P("batch", "seq", None)
    by_column = P(None, BOTH)
    return jax.shard_map(
        on_device,
        mesh=mesh,
        in_specs=(
            rows,
            P("batch", "seq"),
            P("batch", "seq", None, None),
            by_column,
            by_column,
            by_column,
            P(BOTH, None),
            P(),
            rows,
        ),
        out_specs=(
            rows,
            rows,
            P("batch", "seq", None, None),
            by_column,
            by_column,
            by_column,
            P(BOTH, None),
            P(),
        ),
        check_vma=False,
    )
```
